128 devices in a mesh: blk: 8 (over z, core), bfly: 16 (over y, x).
Axes of the slice: x: 4, y: 4, z: 4, core: 2. Of those that a mesh axis runs over, the one named last changes fastest.
Arguments:
- inputs: bfloat16 [8, 65536, 256], P('blk', 'bfly'), may hold values from -6 to 6
- col_basis: bfloat16 [8, 128, 512, 128], P('blk', 'bfly'), may hold values from -0.25 to 0.25
- col_factors: bfloat16 [8, 128, 3, 128, 256], P('blk', 'bfly'), may hold values from -0.375 to 0.375
- row_factors: bfloat16 [8, 128, 3, 128, 256], P('blk', 'bfly'), may hold values from -0.375 to 0.375
- row_basis: bfloat16 [8, 128, 512, 128], P('blk', 'bfly'), may hold values from -0.5 to 0.5
- contrast: float32 [65536], P('bfly'), may hold values from 0.5 to 2
- regroup: int32 [128], replicated, may hold values from 0 to 127, as said below
Outputs:
- result: bfloat16 [8, 65536, 256], P('blk', 'bfly')
- forward: bfloat16 [65536, 256], P(('bfly', 'blk'))
The draws below stay inside these ranges and needn't reach their ends.
Inputs may be any that keep to these rules, and one draw needn't show every extreme that they name: regroup is a permutation of the nodes. Node g lies on index g // 8 of bfly before the midpoint and regroup[g] // 8 after it. No index hands more than 1 of its nodes to one index, and every index hands exactly 1 to some index. The number of nodes that index d hands to index (d + k) mod the size of bfly depends on k only.
All inputs are finite; a program needn't handle non-finite values.
Results may differ from the reference program's by a relative error of at most 0.024.
Values may be sent and summed in bfloat16 or wider, within the bound.
A program may use at most 64 MiB of HBM per device.

```python
import math
import jax
import jax.numpy as jnp
from jax import lax

LEAF = 512
RANK = 128
LEAF_DEV = 8
CAP = 1
COL_LEVELS = 3
ROW_LEVELS = 3
ITERS = 3
NVEC = 256
NODES = 128
ORDER = 65536
BLOCKS = 8


def draw_regroup(key, part):
    sources_count = NODES // LEAF_DEV
    key_counts, key_offsets, key_source, key_target = jax.random.split(jax.random.fold_in(key, 71), 4)
    unit_pos = jnp.repeat(jnp.arange(1, sources_count, dtype=jnp.int32), CAP)
    chosen = jax.random.permutation(key_counts, unit_pos)[:LEAF_DEV - CAP]
    counts = jnp.zeros((sources_count,), jnp.int32).at[0].set(CAP).at[chosen].add(1)
    offsets = jax.random.permutation(key_offsets, sources_count).astype(jnp.int32)
    run_ends = jnp.cumsum(counts)
    unit_ids = jnp.arange(LEAF_DEV, dtype=jnp.int32)
    position = jnp.sum((unit_ids[:, None] >= run_ends[None, :]).astype(jnp.int32), axis=1)
    srcperm = jax.vmap(lambda k: jax.random.permutation(k, LEAF_DEV))(jax.random.split(key_source, sources_count)).astype(jnp.int32)
    slotperm = jax.vmap(lambda k: jax.random.permutation(k, LEAF_DEV))(jax.random.split(key_target, sources_count)).astype(jnp.int32)
    sources = jnp.arange(sources_count, dtype=jnp.int32)
    targets_dev = (sources[:, None] + offsets[position][None, :]) % sources_count
    targets = targets_dev * LEAF_DEV + slotperm[targets_dev, jnp.broadcast_to(unit_ids[None, :], targets_dev.shape)]
    source_index = sources[:, None] * LEAF_DEV + srcperm
    mapping = jnp.zeros((NODES,), jnp.int32).at[source_index.reshape(-1)].set(targets.reshape(-1))
    return mapping


def block_levels(key, dims, cuts, low, top_value):
    loudness = 1.0
    for dim, shards_of in cuts:
        draws = jax.random.uniform(jax.random.fold_in(jax.random.fold_in(key, 6), dim), (shards_of,), jnp.float32, low / len(cuts), top_value / len(cuts))
        loudness = loudness * jnp.repeat(jnp.exp(draws), dims[dim] // shards_of).reshape((-1,) + (1,) * (len(dims) - 1 - dim))
    return loudness


def scatter_about(key, dims, scale, bound, cuts=(), kind=jnp.bfloat16):
    entries = scale * jax.random.normal(key, dims, jnp.float32)
    if cuts:
        entries = entries * block_levels(key, dims, cuts, -0.22, 0.18)
    return jnp.clip(entries, -bound, bound).astype(kind)


def setup_inputs(seed: int = 0) -> dict:
    arg_keys = jax.random.split(jax.random.key(seed), 8)
    inputs = scatter_about(arg_keys[0], (BLOCKS, ORDER, NVEC), 1.0, 6.0, ((0, 8), (1, 16)))
    col_basis = scatter_about(arg_keys[1], (BLOCKS, NODES, LEAF, RANK), LEAF ** -0.5, 0.25, ((0, 8), (1, 16)))
    col_factors = scatter_about(arg_keys[2], (BLOCKS, NODES, COL_LEVELS, RANK, 2 * RANK), (2 * RANK) ** -0.5, 0.375, ((0, 8), (1, 16)))
    row_factors = scatter_about(arg_keys[3], (BLOCKS, NODES, ROW_LEVELS, RANK, 2 * RANK), (2 * RANK) ** -0.5, 0.375, ((0, 8), (1, 16)))
    row_basis = scatter_about(arg_keys[4], (BLOCKS, NODES, LEAF, RANK), RANK ** -0.5, 0.5, ((0, 8), (1, 16)))
    contrast = jnp.clip(jnp.exp(math.log(2.0) - 1.3862944 * jax.random.uniform(arg_keys[5], (ORDER,), jnp.float32) ** block_levels(arg_keys[5], (ORDER,), ((0, 16),), -0.2, 0.2)), 0.5, 2.0)
    regroup = draw_regroup(jax.random.fold_in(arg_keys[7], 71), 0)
    return dict(inputs=inputs, col_basis=col_basis, col_factors=col_factors, row_factors=row_factors, row_basis=row_basis, contrast=contrast, regroup=regroup)


def partner(state_vectors, stride):
    node_count = state_vectors.shape[0]
    grouped = state_vectors.reshape((node_count // (2 * stride), 2, stride) + state_vectors.shape[1:])
    return jnp.flip(grouped, 1).reshape(state_vectors.shape)


def mix_level(state_vectors, mixing_factor, stride):
    stacked_rows = jnp.concatenate([state_vectors, partner(state_vectors, stride)], axis=1).astype(jnp.float32)
    return jnp.einsum("jyz,jzw->jyw", mixing_factor.astype(jnp.float32), stacked_rows).astype(jnp.bfloat16)


def unmix_level(state_vectors, mixing_factor, stride):
    rank_width = state_vectors.shape[1]
    widened_factor = mixing_factor.astype(jnp.float32)
    value_entries = state_vectors.astype(jnp.float32)
    local_portion = jnp.einsum("xaw,xay->xwy", widened_factor[:, :, :rank_width], value_entries)
    partner_portion = jnp.einsum("xaw,xay->xwy", widened_factor[:, :, rank_width:], value_entries)
    return (local_portion + partner(partner_portion, stride)).astype(jnp.bfloat16)


def project(leaf_basis, leaf_rows):
    blocks = leaf_rows.reshape(leaf_basis.shape[0], leaf_basis.shape[1], leaf_rows.shape[-1]).astype(jnp.float32)
    return jnp.einsum("nlr,nlv->nrv", leaf_basis.astype(jnp.float32), blocks).astype(jnp.bfloat16)


def expand(leaf_basis, state_vectors):
    expanded = jnp.einsum("nlr,nrv->nlv", leaf_basis.astype(jnp.float32), state_vectors.astype(jnp.float32))
    return expanded.reshape(-1, state_vectors.shape[-1])


def reference(inputs, col_basis, col_factors, row_factors, row_basis, contrast, regroup):
    current = inputs
    forward = None
    for iteration in range(ITERS):
        def forward_block(pieces):
            leaf_rows, vbasis, col_mix, row_mix, ubasis = pieces
            state_vectors = project(vbasis, leaf_rows)
            for level in range(COL_LEVELS):
                state_vectors = mix_level(state_vectors, col_mix[:, level], 2 ** level)
            state_vectors = jnp.zeros_like(state_vectors).at[regroup].set(state_vectors)
            for level in range(ROW_LEVELS):
                state_vectors = mix_level(state_vectors, row_mix[:, level], 2 ** level)
            return expand(ubasis, state_vectors)

        def accumulate(row_total, pieces):
            return row_total + forward_block(pieces), None

        row_total, unused = lax.scan(accumulate, jnp.zeros((ORDER, NVEC), jnp.float32),
                                     (current, col_basis, col_factors, row_factors, row_basis))
        scaled = row_total * (BLOCKS ** -0.5)
        forward = scaled.astype(jnp.bfloat16)
        weighted = (contrast[:, None] * scaled).astype(jnp.bfloat16)

        def adjoint_block(pieces):
            vbasis, col_mix, row_mix, ubasis = pieces
            state_vectors = project(ubasis, weighted)
            for level in reversed(range(ROW_LEVELS)):
                state_vectors = unmix_level(state_vectors, row_mix[:, level], 2 ** level)
            state_vectors = jnp.take(state_vectors, regroup, axis=0)
            for level in reversed(range(COL_LEVELS)):
                state_vectors = unmix_level(state_vectors, col_mix[:, level], 2 ** level)
            return expand(vbasis, state_vectors).astype(jnp.bfloat16)

        current = lax.map(adjoint_block, (col_basis, col_factors, row_factors, row_basis))
    return current, forward
```

```python
import jax
import jax.numpy as jnp
from jax import lax
from jax.sharding import PartitionSpec as P

CAP = 1
COL_LEVELS = 3
ROW_LEVELS = 3
ITERS = 3


def partner(state_vectors, stride):
    node_count = state_vectors.shape[0]
    grouped = state_vectors.reshape(
        (node_count // (2 * stride), 2, stride) + state_vectors.shape[1:]
    )
    return jnp.flip(grouped, 1).reshape(state_vectors.shape)


def mix_level(state_vectors, mixing_factor, stride):
    stacked_rows = jnp.concatenate([state_vectors, partner(state_vectors, stride)], axis=1)
    return jnp.einsum(
        "jyz,jzw->jyw", mixing_factor, stacked_rows, preferred_element_type=jnp.float32
    ).astype(jnp.bfloat16)


def unmix_level(state_vectors, mixing_factor, stride):
    rank_width = state_vectors.shape[1]
    local_portion = jnp.einsum(
        "xaw,xay->xwy",
        mixing_factor[:, :, :rank_width],
        state_vectors,
        preferred_element_type=jnp.float32,
    )
    partner_portion = jnp.einsum(
        "xaw,xay->xwy",
        mixing_factor[:, :, rank_width:],
        state_vectors,
        preferred_element_type=jnp.float32,
    )
    return (local_portion + partner(partner_portion, stride)).astype(jnp.bfloat16)


def project(leaf_basis, leaf_rows):
    blocks = leaf_rows.reshape(leaf_basis.shape[0], leaf_basis.shape[1], leaf_rows.shape[-1])
    return jnp.einsum(
        "nlr,nlv->nrv", leaf_basis, blocks, preferred_element_type=jnp.float32
    ).astype(jnp.bfloat16)


def expand(leaf_basis, state_vectors):
    expanded = jnp.einsum(
        "nlr,nrv->nlv", leaf_basis, state_vectors, preferred_element_type=jnp.float32
    )
    return expanded.reshape(-1, state_vectors.shape[-1])


def shards(inputs, col_basis, col_factors, row_factors, row_basis, contrast, regroup):
    node_count = col_basis.shape[1]
    leaf_size = col_basis.shape[2]
    devices = lax.axis_size("bfly")
    blocks = lax.axis_size("blk")
    my_index = lax.axis_index("bfly")
    node_ids = jnp.arange(node_count, dtype=jnp.int32)
    owners = (regroup // node_count).reshape(devices, node_count)
    places = (regroup % node_count).reshape(devices, node_count)
    earlier = node_ids[None, :] < node_ids[:, None]
    same_owner = owners[:, :, None] == owners[:, None, :]
    arrival = jnp.sum((same_owner & earlier[None]).astype(jnp.int32), axis=2)
    my_owners = lax.dynamic_index_in_dim(owners, my_index, 0, keepdims=False)
    my_ranks = lax.dynamic_index_in_dim(arrival, my_index, 0, keepdims=False)
    peer_ids = jnp.arange(devices, dtype=jnp.int32)
    seat_ids = jnp.arange(CAP, dtype=jnp.int32)
    send_table = (
        (my_owners[None, None, :] == peer_ids[:, None, None])
        & (my_ranks[None, None, :] == seat_ids[None, :, None])
    ).astype(jnp.bfloat16)
    arrived = (owners == my_index)[:, None, :] & (arrival[:, None, :] == seat_ids[None, :, None])
    take_table = jnp.sum(
        (arrived[None] & (places[None, :, None, :] == node_ids[:, None, None, None])).astype(
            jnp.int32
        ),
        axis=3,
    ).astype(jnp.bfloat16)
    share_rows = node_count * leaf_size // blocks
    share_start = lax.axis_index("blk") * share_rows
    all_basis = lax.all_to_all(row_basis[0], "blk", 0, 0, tiled=True)
    weights = lax.dynamic_slice_in_dim(contrast, share_start, share_rows)
    current = inputs[0]
    forward = None
    for iteration in range(ITERS):
        state_vectors = project(col_basis[0], current)
        for level in range(COL_LEVELS):
            state_vectors = mix_level(state_vectors, col_factors[0, :, level], 2**level)
        outgoing = jnp.einsum(
            "pci,irv->pcrv", send_table, state_vectors, preferred_element_type=jnp.float32
        ).astype(jnp.bfloat16)
        incoming = lax.all_to_all(outgoing, "bfly", split_axis=0, concat_axis=0, tiled=True)
        state_vectors = jnp.einsum(
            "spc,pcrv->srv", take_table, incoming, preferred_element_type=jnp.float32
        ).astype(jnp.bfloat16)
        for level in range(ROW_LEVELS):
            state_vectors = mix_level(state_vectors, row_factors[0, :, level], 2**level)
        gathered = lax.all_to_all(state_vectors, "blk", 0, 0, tiled=True)
        row_share = jnp.einsum(
            "jlr,jrv->lv", all_basis, gathered, preferred_element_type=jnp.float32
        ) * blocks ** (-0.5)
        forward = row_share.astype(jnp.bfloat16)
        weighted = (weights[:, None] * row_share).astype(jnp.bfloat16)
        back = jnp.einsum(
            "jlr,lv->jrv", all_basis, weighted, preferred_element_type=jnp.float32
        ).astype(jnp.bfloat16)
        state_vectors = lax.all_to_all(back, "blk", 0, 0, tiled=True)
        for level in reversed(range(ROW_LEVELS)):
            state_vectors = unmix_level(state_vectors, row_factors[0, :, level], 2**level)
        returning = jnp.einsum(
            "spc,srv->pcrv", take_table, state_vectors, preferred_element_type=jnp.float32
        ).astype(jnp.bfloat16)
        returned = lax.all_to_all(returning, "bfly", split_axis=0, concat_axis=0, tiled=True)
        state_vectors = jnp.einsum(
            "pci,pcrv->irv", send_table, returned, preferred_element_type=jnp.float32
        ).astype(jnp.bfloat16)
        for level in reversed(range(COL_LEVELS)):
            state_vectors = unmix_level(state_vectors, col_factors[0, :, level], 2**level)
        current = expand(col_basis[0], state_vectors).astype(jnp.bfloat16)
    return (current[None], forward)


def solution(mesh):
    placed = (
        P("blk", "bfly", None),
        P("blk", "bfly", None, None),
        P("blk", "bfly", None, None, None),
        P("blk", "bfly", None, None, None),
        P("blk", "bfly", None, None),
        P("bfly"),
        P(),
    )
    return jax.shard_map(
        shards,
        mesh=mesh,
        in_specs=placed,
        out_specs=(P("blk", "bfly", None), P(("bfly", "blk"), None)),
        check_vma=False,
    )
```

```python
import functools

import jax
import jax.numpy as jnp
from jax import lax
from jax.experimental import pallas as pl
from jax.experimental.pallas import tpu as pltpu
from jax.sharding import PartitionSpec as P

ITERS = 3
LEVELS = 3
NC = 4
OFFSETS = (0, 1, 2, 4)
PERIOD = 7
BF16 = jnp.bfloat16
F32 = jnp.float32


def matmul(a, b):
    return lax.dot_general(a, b, (((1,), (0,)), ((), ())), preferred_element_type=F32)


def matmul_t(a, b):
    return lax.dot_general(a, b, (((1,), (1,)), ((), ())), preferred_element_type=F32)


def pairs_of(stride, nodes):
    return [(h, h + stride) for h in range(nodes) if not h & stride]


def mix(states, pair_matrices):
    states = list(states)
    for level in range(LEVELS):
        for q, (h, p) in enumerate(pairs_of(1 << level, len(states))):
            both = jnp.concatenate([states[h], states[p]], axis=1)
            out = matmul_t(both, pair_matrices[level, q]).astype(BF16)
            rank = out.shape[1] // 2
            states[h], states[p] = out[:, :rank], out[:, rank:]
    return states


def unmix(states, pair_matrices):
    states = list(states)
    for level in reversed(range(LEVELS)):
        for q, (h, p) in enumerate(pairs_of(1 << level, len(states))):
            both = jnp.concatenate([states[h], states[p]], axis=1)
            out = matmul(both, pair_matrices[level, q]).astype(BF16)
            rank = out.shape[1] // 2
            states[h], states[p] = out[:, :rank], out[:, rank:]
    return states


def kernel(
    peers, blocks, scale,
    table, x_hbm, col_basis, col_factors, row_factors, row_basis, contrast,
    final, forward,
    x, v, u, w_col, w_row, first, held, landed,
    x1_send, x1_recv, z1_send, z1_recv, z2_send, z2_recv, x2_send, x2_recv,
    x_sem, v_sem, w_sem, own_sem, u_send_sem, u_recv_sem, send_sem, recv_sem,
):
    nodes = v.shape[0]
    rows = x1_send.shape[2]
    rank = x1_send.shape[3]
    d = lax.axis_index("bfly")
    me = lax.axis_index("blk")

    def bfly_peer(k):
        return {"bfly": lax.rem(d + k, peers)}

    def blk_peer(k):
        return {"blk": lax.rem(me + k, blocks)}

    barrier = pltpu.get_barrier_semaphore()

    @pl.loop(1, peers)
    def _(k):
        pl.semaphore_signal(barrier, inc=1, device_id=bfly_peer(k))

    @pl.loop(1, blocks)
    def _(k):
        pl.semaphore_signal(barrier, inc=1, device_id=blk_peer(k))

    @pl.loop(0, nodes)
    def _(g):
        pltpu.make_async_copy(x_hbm.at[g], x.at[g], x_sem.at[g]).start()
        pltpu.make_async_copy(col_basis.at[g], v.at[g], v_sem.at[g]).start()

    for which, (source, target) in enumerate(((col_factors, w_col), (row_factors, w_row))):
        for level in range(LEVELS):
            for q, (h, p) in enumerate(pairs_of(1 << level, nodes)):
                for node, row, own, other in ((h, 0, 0, rank), (p, rank, rank, 0)):
                    for start, column in ((0, own), (rank, other)):
                        pltpu.make_async_copy(
                            source.at[node, level, :, pl.ds(start, rank)],
                            target.at[level, q, pl.ds(row, rank), pl.ds(column, rank)],
                            w_sem.at[which],
                        ).start()
    own_basis = pltpu.make_async_copy(row_basis.at[me], u.at[0], own_sem)
    own_basis.start()

    pl.semaphore_wait(barrier, peers + blocks - 2)

    def basis_copy(k):
        target = lax.rem(me + k, blocks)
        return pltpu.make_async_remote_copy(
            src_ref=row_basis.at[target], dst_ref=u.at[blocks - k],
            send_sem=u_send_sem.at[k], recv_sem=u_recv_sem.at[blocks - k],
            device_id={"blk": target},
        )

    @pl.loop(1, blocks)
    def _(k):
        basis_copy(k).start()

    def send_bfly(which, send, recv, c):
        @pl.loop(1, peers)
        def _(k):
            pltpu.make_async_remote_copy(
                src_ref=send.at[c, k], dst_ref=recv.at[c, k],
                send_sem=send_sem.at[which, c], recv_sem=recv_sem.at[which, c],
                device_id=bfly_peer(k),
            ).start()

    def send_blk(which, send, recv, c):
        recv[c, 0] = send[c, 0]

        @pl.loop(1, blocks)
        def _(k):
            pltpu.make_async_remote_copy(
                src_ref=send.at[c, k], dst_ref=recv.at[c, blocks - k],
                send_sem=send_sem.at[which, c], recv_sem=recv_sem.at[which, c],
                device_id=blk_peer(k),
            ).start()

    def wait_all(which, send, recv, c):
        count = send.shape[1] - 1
        part = recv.at[c, pl.ds(1, count)]
        pltpu.make_async_copy(part, part, recv_sem.at[which, c]).wait()
        part = send.at[c, pl.ds(1, count)]
        pltpu.make_async_copy(part, part, send_sem.at[which, c]).wait()

    def route(which, line, states, send, recv, c):
        for i, state in enumerate(states):
            held[i] = state
        recv[c, 0] = held[table[line, 0]]
        for k in range(1, peers):
            send[c, k] = held[table[line, k]]
        send_bfly(which, send, recv, c)

    def arrived(line, recv, c):
        for k in range(peers):
            landed[k] = recv[c, k]
        return [landed[table[line, i]] for i in range(nodes)]

    @pl.loop(0, nodes)
    def _(g):
        pltpu.make_async_copy(x_hbm.at[g], x.at[g], x_sem.at[g]).wait()
        pltpu.make_async_copy(col_basis.at[g], v.at[g], v_sem.at[g]).wait()
        leaf = lax.dot_general(
            x[g], v[g], (((0,), (0,)), ((), ())), preferred_element_type=F32
        ).astype(BF16)
        for c in range(NC):
            first[c, g] = leaf[c * rows : (c + 1) * rows]

    pltpu.make_async_copy(w_col, w_col, w_sem.at[0]).wait()

    @pl.loop(0, NC)
    def _(c):
        states = mix([first[c, g] for g in range(nodes)], w_col)
        route(0, 0, states, x1_send, x1_recv, c)

    pltpu.make_async_copy(w_row, w_row, w_sem.at[1]).wait()

    def phase2(c):
        wait_all(0, x1_send, x1_recv, c)
        states = mix(arrived(1, x1_recv, c), w_row)
        for h in range(nodes):
            z1_send[c, lax.rem(h - me + blocks, blocks)] = states[h]
        send_blk(1, z1_send, z1_recv, c)

    def phase3(c):
        wait_all(1, z1_send, z1_recv, c)
        states = jnp.concatenate([z1_recv[c, j] for j in range(blocks)], axis=1)
        basis = jnp.concatenate([u[j] for j in range(blocks)], axis=1)
        weighted = (contrast[...] * (matmul_t(states, basis) * scale)).astype(BF16)
        back = matmul(weighted, basis).astype(BF16)
        for j in range(blocks):
            z2_send[c, j] = back[:, j * rank : (j + 1) * rank]
        send_blk(2, z2_send, z2_recv, c)

    def phase4(c):
        wait_all(2, z2_send, z2_recv, c)
        states = unmix(
            [z2_recv[c, lax.rem(h - me + blocks, blocks)] for h in range(nodes)], w_row
        )
        route(3, 2, states, x2_send, x2_recv, c)

    def phase5(c, t):
        wait_all(3, x2_send, x2_recv, c)
        states = unmix(arrived(3, x2_recv, c), w_col)

        @pl.when(t == ITERS - 1)
        def _():
            for i in range(nodes):
                final[i, pl.ds(pl.multiple_of(c * rows, rows), rows)] = states[i]

        @pl.when(t < ITERS - 1)
        def _():
            leaves = []
            for i in range(nodes):
                result = matmul_t(states[i], v[i]).astype(BF16)
                leaves.append(matmul(result, v[i]).astype(BF16))
            route(0, 0, mix(leaves, w_col), x1_send, x1_recv, c)

    @pl.loop(0, PERIOD * (ITERS - 1) + NC + OFFSETS[3])
    def _(step):
        def place(offset):
            u_step = step - offset
            shifted = u_step + PERIOD
            t = shifted // PERIOD - 1
            c = lax.rem(shifted, PERIOD)
            return t, c, (u_step >= 0) & (c < NC) & (t < ITERS)

        t, c, live = place(OFFSETS[0])

        @pl.when(live)
        def _():
            phase2(c)

        t, c, live = place(OFFSETS[1])

        @pl.when(live & (c == 0) & (t == 0))
        def _():
            own_basis.wait()

            @pl.loop(1, blocks)
            def _(k):
                basis_copy(k).wait_send()
                basis_copy(blocks - k).wait_recv()

        @pl.when(live)
        def _():
            phase3(c)

        t, c, live = place(OFFSETS[2])

        @pl.when(live)
        def _():
            phase4(c)

        @pl.when(live & (c == NC - 1) & (t == ITERS - 1))
        def _():
            states = jnp.concatenate(
                [
                    jnp.concatenate([z1_recv[e, j] for j in range(blocks)], axis=1)
                    for e in range(NC)
                ],
                axis=0,
            )
            basis = jnp.concatenate([u[j] for j in range(blocks)], axis=1)
            forward[...] = (matmul_t(basis, states) * scale).astype(BF16)

        t, c, live = place(OFFSETS[3])

        @pl.when(live)
        def _():
            phase5(c, t)


def expand_kernel(basis, state, out):
    out[0] = matmul_t(basis[0], state[0]).astype(BF16)


def shards(inputs, col_basis, col_factors, row_factors, row_basis, contrast, regroup):
    _, nodes, leaf, rank = col_basis.shape
    vectors = inputs.shape[-1]
    peers = lax.axis_size("bfly")
    blocks = lax.axis_size("blk")
    d = lax.axis_index("bfly")
    me = lax.axis_index("blk")
    rows = vectors // NC

    places = jnp.arange(nodes * peers, dtype=jnp.int32)
    offsets = jnp.arange(peers, dtype=jnp.int32)
    owner = regroup // nodes
    source = places // nodes
    mine = lax.dynamic_slice_in_dim(owner, d * nodes, nodes)
    local = jnp.arange(nodes, dtype=jnp.int32)
    there = lax.rem(mine - d + peers, peers)
    go = jnp.sum(jnp.where(there[None] == offsets[:, None], local[None], 0), axis=1)
    back_from = lax.rem(d - mine + peers, peers)
    arrives = regroup[None, :] == (d * nodes + local)[:, None]
    origin = jnp.sum(jnp.where(arrives, source[None, :], 0), axis=1)
    come_from = lax.rem(d - origin + peers, peers)
    back_to = lax.rem(origin - d + peers, peers)
    back_go = jnp.sum(jnp.where(back_to[None] == offsets[:, None], local[None], 0), axis=1)
    pad = jnp.zeros((peers - nodes,), jnp.int32)
    table = jnp.stack(
        [go, jnp.concatenate([come_from, pad]), back_go, jnp.concatenate([back_from, pad])]
    )
    weights = lax.dynamic_slice_in_dim(contrast, me * leaf, leaf).reshape(1, leaf)

    hbm = pl.BlockSpec(memory_space=pl.ANY)
    vmem = pl.BlockSpec(memory_space=pltpu.VMEM)
    wide = (NC, peers, rows, rank)
    narrow = (NC, blocks, rows, rank)
    final, forward = pl.pallas_call(
        functools.partial(kernel, peers, blocks, blocks ** (-0.5)),
        out_shape=(
            jax.ShapeDtypeStruct((nodes, vectors, rank), BF16),
            jax.ShapeDtypeStruct((leaf, vectors), BF16),
        ),
        in_specs=[pl.BlockSpec(memory_space=pltpu.SMEM), hbm, hbm, hbm, hbm, hbm, vmem],
        out_specs=(vmem, vmem),
        scratch_shapes=[
            pltpu.VMEM((nodes, leaf, vectors), BF16),
            pltpu.VMEM((nodes, leaf, rank), BF16),
            pltpu.VMEM((blocks, leaf, rank), BF16),
            pltpu.VMEM((LEVELS, nodes // 2, 2 * rank, 2 * rank), BF16),
            pltpu.VMEM((LEVELS, nodes // 2, 2 * rank, 2 * rank), BF16),
            pltpu.VMEM((NC, nodes, rows, rank), BF16),
            pltpu.VMEM((nodes, rows, rank), BF16),
            pltpu.VMEM((peers, rows, rank), BF16),
            pltpu.VMEM(wide, BF16),
            pltpu.VMEM(wide, BF16),
            pltpu.VMEM(narrow, BF16),
            pltpu.VMEM(narrow, BF16),
            pltpu.VMEM(narrow, BF16),
            pltpu.VMEM(narrow, BF16),
            pltpu.VMEM(wide, BF16),
            pltpu.VMEM(wide, BF16),
            pltpu.SemaphoreType.DMA((nodes,)),
            pltpu.SemaphoreType.DMA((nodes,)),
            pltpu.SemaphoreType.DMA((2,)),
            pltpu.SemaphoreType.DMA,
            pltpu.SemaphoreType.DMA((blocks,)),
            pltpu.SemaphoreType.DMA((blocks,)),
            pltpu.SemaphoreType.DMA((4, NC)),
            pltpu.SemaphoreType.DMA((4, NC)),
        ],
        compiler_params=pltpu.CompilerParams(collective_id=0, has_side_effects=True),
        name="butterfly",
    )(
        table,
        inputs.reshape(nodes, leaf, vectors),
        col_basis[0],
        col_factors[0],
        row_factors[0],
        row_basis[0],
        weights,
    )
    result = pl.pallas_call(
        expand_kernel,
        grid=(nodes,),
        out_shape=jax.ShapeDtypeStruct((nodes, leaf, vectors), BF16),
        in_specs=[
            pl.BlockSpec((1, leaf, rank), lambda g: (g, 0, 0)),
            pl.BlockSpec((1, vectors, rank), lambda g: (g, 0, 0)),
        ],
        out_specs=pl.BlockSpec((1, leaf, vectors), lambda g: (g, 0, 0)),
        name="expand",
    )(col_basis[0], final)
    return result.reshape(inputs.shape), forward


def solution(mesh):
    placed = (
        P("blk", "bfly", None),
        P("blk", "bfly", None, None),
        P("blk", "bfly", None, None, None),
        P("blk", "bfly", None, None, None),
        P("blk", "bfly", None, None),
        P("bfly"),
        P(),
    )
    return jax.shard_map(
        shards,
        mesh=mesh,
        in_specs=placed,
        out_specs=(P("blk", "bfly", None), P(("bfly", "blk"), None)),
        check_vma=False,
    )
```

```python
import functools

import jax
import jax.numpy as jnp
from jax import lax
from jax.experimental import pallas as pl
from jax.experimental.pallas import tpu as pltpu
from jax.sharding import PartitionSpec as P

ITERS = 3
LEVELS = 3
NC = 4
OFFSETS = (0, 1, 2, 3)
PERIOD = 5
BF16 = jnp.bfloat16
F32 = jnp.float32


def matmul(a, b):
    return lax.dot_general(a, b, (((1,), (0,)), ((), ())), preferred_element_type=F32)


def matmul_t(a, b):
    return lax.dot_general(a, b, (((1,), (1,)), ((), ())), preferred_element_type=F32)


def pairs_of(stride, nodes):
    return [(h, h + stride) for h in range(nodes) if not h & stride]


def mix_level(states, pair_matrices, level):
    states = list(states)
    for q, (h, p) in enumerate(pairs_of(1 << level, len(states))):
        both = jnp.concatenate([states[h], states[p]], axis=1)
        out = matmul_t(both, pair_matrices[level, q]).astype(BF16)
        rank = out.shape[1] // 2
        states[h], states[p] = out[:, :rank], out[:, rank:]
    return states


def unmix_level(states, pair_matrices, level):
    states = list(states)
    for q, (h, p) in enumerate(pairs_of(1 << level, len(states))):
        both = jnp.concatenate([states[h], states[p]], axis=1)
        out = matmul(both, pair_matrices[level, q]).astype(BF16)
        rank = out.shape[1] // 2
        states[h], states[p] = out[:, :rank], out[:, rank:]
    return states


def mix(states, pair_matrices, first=0):
    for level in range(first, LEVELS):
        states = mix_level(states, pair_matrices, level)
    return states


def unmix(states, pair_matrices, last=0):
    for level in reversed(range(last, LEVELS)):
        states = unmix_level(states, pair_matrices, level)
    return states


def node_at(offsets, k):
    place = jnp.int32(0)
    for i, offset in enumerate(offsets):
        place = jnp.where(offset == k, i, place)
    return place


def kernel(
    peers, blocks, scale,
    regroup, x_hbm, col_basis, col_factors, row_factors, row_basis, all_contrast,
    final, forward,
    x, v, u, w_col, w_row, w_turn, contrast, first, held, landed, table,
    x1_send, x1_recv, z1_send, z1_recv, z2_send, z2_recv, x2_send, x2_recv,
    x_sem, v_sem, w_sem, own_sem, u_send_sem, u_recv_sem, send_sem, recv_sem,
):
    nodes = v.shape[0]
    rows = x1_send.shape[2]
    rank = x1_send.shape[3]
    d = lax.axis_index("bfly")
    me = lax.axis_index("blk")

    def bfly_peer(k):
        return {"bfly": lax.rem(d + k, peers)}

    def blk_peer(k):
        return {"blk": lax.rem(me + k, blocks)}

    barrier = pltpu.get_barrier_semaphore()

    @pl.loop(0, nodes)
    def _(g):
        pltpu.make_async_copy(x_hbm.at[g], x.at[g], x_sem.at[g]).start()
        pltpu.make_async_copy(col_basis.at[g], v.at[g], v_sem.at[g]).start()

    @pl.loop(1, peers)
    def _(k):
        pl.semaphore_signal(barrier, inc=1, device_id=bfly_peer(k))

    @pl.loop(1, blocks)
    def _(k):
        pl.semaphore_signal(barrier, inc=1, device_id=blk_peer(k))

    def load_pairs(which, source, target):
        for level in range(LEVELS):
            for q, (h, p) in enumerate(pairs_of(1 << level, nodes)):
                moves = (
                    (h, 0, 2 * rank, 0, 0), (p, 0, rank, rank, rank), (p, rank, rank, rank, 0)
                )
                for node, start, width, row, column in moves:
                    pltpu.make_async_copy(
                        source.at[node, level, :, pl.ds(start, width)],
                        target.at[level, q, pl.ds(row, rank), pl.ds(column, width)],
                        w_sem.at[which],
                    ).start()

    load_pairs(0, col_factors, w_col)
    own_basis = pltpu.make_async_copy(row_basis.at[me], u.at[0], own_sem)
    own_basis.start()

    owners = [regroup[d * nodes + i] // nodes for i in range(nodes)]
    there = [lax.rem(owner - d + peers, peers) for owner in owners]
    for k in range(peers):
        table[0, k] = node_at(there, k)
    for i in range(nodes):
        table[3, i] = lax.rem(d - owners[i] + peers, peers)

    pl.semaphore_wait(barrier, peers + blocks - 2)

    def basis_copy(k):
        target = lax.rem(me + k, blocks)
        return pltpu.make_async_remote_copy(
            src_ref=row_basis.at[target], dst_ref=u.at[blocks - k],
            send_sem=u_send_sem.at[k], recv_sem=u_recv_sem.at[blocks - k],
            device_id={"blk": target},
        )

    @pl.loop(1, blocks)
    def _(k):
        basis_copy(k).start()

    def send_bfly(which, send, recv, c):
        @pl.loop(1, peers)
        def _(k):
            pltpu.make_async_remote_copy(
                src_ref=send.at[c, k], dst_ref=recv.at[c, k],
                send_sem=send_sem.at[which, c], recv_sem=recv_sem.at[which, c],
                device_id=bfly_peer(k),
            ).start()

    def send_blk(which, send, recv, c):
        recv[c, 0] = send[c, 0]

        @pl.loop(1, blocks)
        def _(k):
            pltpu.make_async_remote_copy(
                src_ref=send.at[c, k], dst_ref=recv.at[c, blocks - k],
                send_sem=send_sem.at[which, c], recv_sem=recv_sem.at[which, c],
                device_id=blk_peer(k),
            ).start()

    def wait_all(which, send, recv, c):
        count = send.shape[1] - 1
        part = recv.at[c, pl.ds(1, count)]
        pltpu.make_async_copy(part, part, recv_sem.at[which, c]).wait()
        part = send.at[c, pl.ds(1, count)]
        pltpu.make_async_copy(part, part, send_sem.at[which, c]).wait()

    def route(which, line, states, send, recv, c):
        for i, state in enumerate(states):
            held[i] = state
        recv[c, 0] = held[table[line, 0]]
        for k in range(1, peers):
            send[c, k] = held[table[line, k]]
        send_bfly(which, send, recv, c)

    def arrived(line, recv, c):
        for k in range(peers):
            landed[k] = recv[c, k]
        return [landed[table[line, i]] for i in range(nodes)]

    @pl.loop(0, nodes)
    def _(g):
        pltpu.make_async_copy(x_hbm.at[g], x.at[g], x_sem.at[g]).wait()
        pltpu.make_async_copy(col_basis.at[g], v.at[g], v_sem.at[g]).wait()
        leaf = lax.dot_general(
            x[g], v[g], (((0,), (0,)), ((), ())), preferred_element_type=F32
        ).astype(BF16)
        for c in range(NC):
            first[c, g] = leaf[c * rows : (c + 1) * rows]

    pltpu.make_async_copy(w_col, w_col, w_sem.at[0]).wait()

    @pl.loop(0, NC)
    def _(c):
        states = mix([first[c, g] for g in range(nodes)], w_col)
        route(0, 0, states, x1_send, x1_recv, c)

    load_pairs(1, row_factors, w_row)

    def seek(g, origins):
        target = regroup[g]
        source = g // nodes
        hit = target // nodes == d
        place = lax.rem(target, nodes)
        return tuple(
            jnp.where(hit & (place == h), source, origin) for h, origin in enumerate(origins)
        )

    origins = lax.fori_loop(0, nodes * peers, seek, (jnp.int32(0),) * nodes)
    back_to = [lax.rem(origin - d + peers, peers) for origin in origins]
    for k in range(peers):
        table[2, k] = node_at(back_to, k)
    for h in range(nodes):
        table[1, h] = lax.rem(d - origins[h] + peers, peers)

    for q, pair in enumerate(pairs_of(1, nodes)):
        outer = w_col[0, q]
        halves = []
        for half, g in enumerate(pair):
            gram = lax.dot_general(
                v[g], v[g], (((0,), (0,)), ((), ())), preferred_element_type=F32
            ).astype(BF16)
            halves.append(matmul(outer[:, half * rank : (half + 1) * rank], gram).astype(BF16))
        w_turn[q] = matmul_t(jnp.concatenate(halves, axis=1), outer).astype(BF16)

    lines = contrast.shape[1] // rank
    contrast[...] = jnp.concatenate(
        [all_contrast[pl.ds(me * lines + i, 1)] for i in range(lines)], axis=1
    )
    pltpu.make_async_copy(w_row, w_row, w_sem.at[1]).wait()

    def phase2(c):
        wait_all(0, x1_send, x1_recv, c)
        states = mix(arrived(1, x1_recv, c), w_row)
        for h in range(nodes):
            z1_send[c, lax.rem(h - me + blocks, blocks)] = states[h]
        send_blk(1, z1_send, z1_recv, c)

    def phase3(c):
        wait_all(1, z1_send, z1_recv, c)
        states = jnp.concatenate([z1_recv[c, j] for j in range(blocks)], axis=1)
        basis = jnp.concatenate([u[j] for j in range(blocks)], axis=1)
        weighted = (contrast[...] * scale * matmul_t(states, basis)).astype(BF16)
        back = matmul(weighted, basis).astype(BF16)
        for j in range(blocks):
            z2_send[c, j] = back[:, j * rank : (j + 1) * rank]
        send_blk(2, z2_send, z2_recv, c)

    def phase4(c):
        wait_all(2, z2_send, z2_recv, c)
        states = unmix(
            [z2_recv[c, lax.rem(h - me + blocks, blocks)] for h in range(nodes)], w_row
        )
        route(3, 2, states, x2_send, x2_recv, c)

    def phase5(c, t):
        wait_all(3, x2_send, x2_recv, c)
        states = unmix(arrived(3, x2_recv, c), w_col, 1)

        @pl.when(t == ITERS - 1)
        def _():
            last = unmix_level(states, w_col, 0)
            for i in range(nodes):
                final[i, pl.ds(pl.multiple_of(c * rows, rows), rows)] = last[i]

        @pl.when(t < ITERS - 1)
        def _():
            turned = list(states)
            for q, (h, p) in enumerate(pairs_of(1, nodes)):
                both = jnp.concatenate([states[h], states[p]], axis=1)
                out = matmul(both, w_turn[q]).astype(BF16)
                turned[h], turned[p] = out[:, :rank], out[:, rank:]
            route(0, 0, mix(turned, w_col, 1), x1_send, x1_recv, c)

    @pl.loop(0, PERIOD * (ITERS - 1) + NC + OFFSETS[3])
    def _(step):
        def place(offset):
            u_step = step - offset
            shifted = u_step + PERIOD
            t = shifted // PERIOD - 1
            c = lax.rem(shifted, PERIOD)
            return t, c, (u_step >= 0) & (c < NC) & (t < ITERS)

        t, c, live = place(OFFSETS[0])

        @pl.when(live)
        def _():
            phase2(c)

        t, c, live = place(OFFSETS[1])

        @pl.when(live & (c == 0) & (t == 0))
        def _():
            own_basis.wait()

            @pl.loop(1, blocks)
            def _(k):
                basis_copy(k).wait_send()
                basis_copy(blocks - k).wait_recv()

        @pl.when(live)
        def _():
            phase3(c)

        t, c, live = place(OFFSETS[2])

        @pl.when(live)
        def _():
            phase4(c)

        @pl.when(live & (c == NC - 1) & (t == ITERS - 1))
        def _():
            states = jnp.concatenate(
                [
                    jnp.concatenate([z1_recv[e, j] for j in range(blocks)], axis=1)
                    for e in range(NC)
                ],
                axis=0,
            )
            basis = jnp.concatenate([u[j] for j in range(blocks)], axis=1)
            forward[...] = (matmul_t(basis, states) * scale).astype(BF16)

        t, c, live = place(OFFSETS[3])

        @pl.when(live)
        def _():
            phase5(c, t)


def expand_kernel(basis_hbm, state_hbm, out_hbm, basis, state, out, in_sem, out_sem):
    nodes = basis.shape[0]

    def load(g):
        return (
            pltpu.make_async_copy(basis_hbm.at[g], basis.at[g], in_sem.at[0, g]),
            pltpu.make_async_copy(state_hbm.at[g], state.at[g], in_sem.at[1, g]),
        )

    def store(g):
        return pltpu.make_async_copy(out.at[g], out_hbm.at[g], out_sem.at[g])

    for g in range(nodes):
        for copy in load(g):
            copy.start()
    for g in range(nodes):
        for copy in load(g):
            copy.wait()
        out[g] = matmul_t(basis[g], state[g]).astype(BF16)
        store(g).start()
    for g in range(nodes):
        store(g).wait()


def shards(inputs, col_basis, col_factors, row_factors, row_basis, contrast, regroup):
    _, nodes, leaf, rank = col_basis.shape
    vectors = inputs.shape[-1]
    peers = lax.axis_size("bfly")
    blocks = lax.axis_size("blk")
    rows = vectors // NC
    hbm = pl.BlockSpec(memory_space=pl.ANY)
    vmem = pl.BlockSpec(memory_space=pltpu.VMEM)
    wide = (NC, peers, rows, rank)
    narrow = (NC, blocks, rows, rank)
    final, forward = pl.pallas_call(
        functools.partial(kernel, peers, blocks, blocks ** (-0.5)),
        out_shape=(
            jax.ShapeDtypeStruct((nodes, vectors, rank), BF16),
            jax.ShapeDtypeStruct((leaf, vectors), BF16),
        ),
        in_specs=[pl.BlockSpec(memory_space=pltpu.SMEM), hbm, hbm, hbm, hbm, hbm, vmem],
        out_specs=(vmem, vmem),
        scratch_shapes=[
            pltpu.VMEM((nodes, leaf, vectors), BF16),
            pltpu.VMEM((nodes, leaf, rank), BF16),
            pltpu.VMEM((blocks, leaf, rank), BF16),
            pltpu.VMEM((LEVELS, nodes // 2, 2 * rank, 2 * rank), BF16),
            pltpu.VMEM((LEVELS, nodes // 2, 2 * rank, 2 * rank), BF16),
            pltpu.VMEM((nodes // 2, 2 * rank, 2 * rank), BF16),
            pltpu.VMEM((1, leaf), F32),
            pltpu.VMEM((NC, nodes, rows, rank), BF16),
            pltpu.VMEM((nodes, rows, rank), BF16),
            pltpu.VMEM((peers, rows, rank), BF16),
            pltpu.SMEM((4, peers), jnp.int32),
            pltpu.VMEM(wide, BF16),
            pltpu.VMEM(wide, BF16),
            pltpu.VMEM(narrow, BF16),
            pltpu.VMEM(narrow, BF16),
            pltpu.VMEM(narrow, BF16),
            pltpu.VMEM(narrow, BF16),
            pltpu.VMEM(wide, BF16),
            pltpu.VMEM(wide, BF16),
            pltpu.SemaphoreType.DMA((nodes,)),
            pltpu.SemaphoreType.DMA((nodes,)),
            pltpu.SemaphoreType.DMA((2,)),
            pltpu.SemaphoreType.DMA,
            pltpu.SemaphoreType.DMA((blocks,)),
            pltpu.SemaphoreType.DMA((blocks,)),
            pltpu.SemaphoreType.DMA((4, NC)),
            pltpu.SemaphoreType.DMA((4, NC)),
        ],
        compiler_params=pltpu.CompilerParams(collective_id=0, has_side_effects=True),
        name="butterfly",
    )(
        regroup,
        inputs.reshape(nodes, leaf, vectors),
        col_basis[0],
        col_factors[0],
        row_factors[0],
        row_basis[0],
        contrast.reshape(-1, rank),
    )
    result = pl.pallas_call(
        expand_kernel,
        out_shape=jax.ShapeDtypeStruct((nodes, leaf, vectors), BF16),
        in_specs=[hbm, hbm],
        out_specs=hbm,
        scratch_shapes=[
            pltpu.VMEM((nodes, leaf, rank), BF16),
            pltpu.VMEM((nodes, vectors, rank), BF16),
            pltpu.VMEM((nodes, leaf, vectors), BF16),
            pltpu.SemaphoreType.DMA((2, nodes)),
            pltpu.SemaphoreType.DMA((nodes,)),
        ],
        name="expand",
    )(col_basis[0], final)
    return result.reshape(inputs.shape), forward


def solution(mesh):
    placed = (
        P("blk", "bfly", None),
        P("blk", "bfly", None, None),
        P("blk", "bfly", None, None, None),
        P("blk", "bfly", None, None, None),
        P("blk", "bfly", None, None),
        P("bfly"),
        P(),
    )
    return jax.shard_map(
        shards,
        mesh=mesh,
        in_specs=placed,
        out_specs=(P("blk", "bfly", None), P(("bfly", "blk"), None)),
        check_vma=False,
    )
```

```python
import functools

import jax
import jax.numpy as jnp
from jax import lax
from jax.experimental import pallas as pl
from jax.experimental.pallas import tpu as pltpu
from jax.sharding import PartitionSpec as P

LEVELS = 3
NC = 4
ORDER = (
    20, 21, 22, 30, 31, 32, 40, 23, 41, 42, 50, 33, 51, 43, 20, 52,
    21, 30, 53, 31, 40, 22, 41, 23, 32, 50, 33, 42, 43, 51, 20, 52,
    30, 53, 21, 40, 22, 31, 23, 32, 41, 33, 42, 43, 50, 51, 52, 53,
)
BITS = 5
PER_WORD = 6
FORWARD = 20
TURN = 24
BF16 = jnp.bfloat16
F32 = jnp.float32


def matmul(a, b):
    return lax.dot_general(a, b, (((1,), (0,)), ((), ())), preferred_element_type=F32)


def matmul_t(a, b):
    return lax.dot_general(a, b, (((1,), (1,)), ((), ())), preferred_element_type=F32)


def pairs_of(stride, nodes):
    return [(h, h + stride) for h in range(nodes) if not h & stride]


def mix_level(states, pair_matrices, level):
    states = list(states)
    for q, (h, p) in enumerate(pairs_of(1 << level, len(states))):
        both = jnp.concatenate([states[h], states[p]], axis=1)
        out = matmul_t(both, pair_matrices[level, q]).astype(BF16)
        rank = out.shape[1] // 2
        states[h], states[p] = out[:, :rank], out[:, rank:]
    return states


def unmix_level(states, pair_matrices, level):
    states = list(states)
    for q, (h, p) in enumerate(pairs_of(1 << level, len(states))):
        both = jnp.concatenate([states[h], states[p]], axis=1)
        out = matmul(both, pair_matrices[level, q]).astype(BF16)
        rank = out.shape[1] // 2
        states[h], states[p] = out[:, :rank], out[:, rank:]
    return states


def mix(states, pair_matrices, first=0):
    for level in range(first, LEVELS):
        states = mix_level(states, pair_matrices, level)
    return states


def unmix(states, pair_matrices, last=0):
    for level in reversed(range(last, LEVELS)):
        states = unmix_level(states, pair_matrices, level)
    return states


def node_at(offsets, k):
    place = jnp.int32(0)
    for i, offset in enumerate(offsets):
        place = jnp.where(offset == k, i, place)
    return place


def steps():
    codes = []
    for i, entry in enumerate(ORDER):
        phase, c = divmod(entry, 10)
        if phase == 5 and TURN not in codes:
            codes.append(TURN)
        left = ORDER[i + 1 :].count(entry)
        codes.append(4 * (phase - 2) + c + (4 if phase == 5 and not left else 0))
        if phase == 4 and not any(later // 10 == 4 for later in ORDER[i + 1 :]):
            codes.append(FORWARD)
    return codes


def kernel(
    peers, blocks, scale,
    regroup, x_hbm, col_basis, col_factors, row_factors, row_basis, all_contrast,
    final, forward,
    x, v, u, w_col, w_row, w_turn, contrast, first, held, landed, table,
    x1_send, x1_recv, z1_send, z1_recv, z2_send, z2_recv, x2_send, x2_recv,
    x_sem, v_sem, w_sem, own_sem, u_send_sem, u_recv_sem, send_sem, recv_sem,
):
    nodes = v.shape[0]
    rows = x1_send.shape[2]
    rank = x1_send.shape[3]
    d = lax.axis_index("bfly")
    me = lax.axis_index("blk")

    def bfly_peer(k):
        return {"bfly": lax.rem(d + k, peers)}

    def blk_peer(k):
        return {"blk": lax.rem(me + k, blocks)}

    barrier = pltpu.get_barrier_semaphore()

    @pl.loop(0, nodes)
    def _(g):
        pltpu.make_async_copy(x_hbm.at[g], x.at[g], x_sem.at[g]).start()
        pltpu.make_async_copy(col_basis.at[g], v.at[g], v_sem.at[g]).start()

    @pl.loop(1, peers)
    def _(k):
        pl.semaphore_signal(barrier, inc=1, device_id=bfly_peer(k))

    @pl.loop(1, blocks)
    def _(k):
        pl.semaphore_signal(barrier, inc=1, device_id=blk_peer(k))

    def load_pairs(which, source, target):
        for level in range(LEVELS):
            for q, (h, p) in enumerate(pairs_of(1 << level, nodes)):
                moves = (
                    (h, 0, 2 * rank, 0, 0), (p, 0, rank, rank, rank), (p, rank, rank, rank, 0)
                )
                for node, start, width, row, column in moves:
                    pltpu.make_async_copy(
                        source.at[node, level, :, pl.ds(start, width)],
                        target.at[level, q, pl.ds(row, rank), pl.ds(column, width)],
                        w_sem.at[which],
                    ).start()

    load_pairs(0, col_factors, w_col)
    own_basis = pltpu.make_async_copy(row_basis.at[me], u.at[0], own_sem)
    own_basis.start()

    owners = [regroup[d * nodes + i] // nodes for i in range(nodes)]
    there = [lax.rem(owner - d + peers, peers) for owner in owners]
    for k in range(peers):
        table[0, k] = node_at(there, k)
    for i in range(nodes):
        table[3, i] = lax.rem(d - owners[i] + peers, peers)

    pl.semaphore_wait(barrier, peers + blocks - 2)

    def basis_copy(k):
        target = lax.rem(me + k, blocks)
        return pltpu.make_async_remote_copy(
            src_ref=row_basis.at[target], dst_ref=u.at[blocks - k],
            send_sem=u_send_sem.at[k], recv_sem=u_recv_sem.at[blocks - k],
            device_id={"blk": target},
        )

    @pl.loop(1, blocks)
    def _(k):
        basis_copy(k).start()

    def send_bfly(which, send, recv, c):
        @pl.loop(1, peers)
        def _(k):
            pltpu.make_async_remote_copy(
                src_ref=send.at[c, k], dst_ref=recv.at[c, k],
                send_sem=send_sem.at[which, c], recv_sem=recv_sem.at[which, c],
                device_id=bfly_peer(k),
            ).start()

    def send_blk(which, send, recv, c):
        recv[c, 0] = send[c, 0]

        @pl.loop(1, blocks)
        def _(k):
            pltpu.make_async_remote_copy(
                src_ref=send.at[c, k], dst_ref=recv.at[c, blocks - k],
                send_sem=send_sem.at[which, c], recv_sem=recv_sem.at[which, c],
                device_id=blk_peer(k),
            ).start()

    def wait_all(which, send, recv, c):
        count = send.shape[1] - 1
        part = recv.at[c, pl.ds(1, count)]
        pltpu.make_async_copy(part, part, recv_sem.at[which, c]).wait()
        part = send.at[c, pl.ds(1, count)]
        pltpu.make_async_copy(part, part, send_sem.at[which, c]).wait()

    def route(which, line, states, send, recv, c):
        for i, state in enumerate(states):
            held[i] = state
        recv[c, 0] = held[table[line, 0]]
        for k in range(1, peers):
            send[c, k] = held[table[line, k]]
        send_bfly(which, send, recv, c)

    def arrived(line, recv, c):
        for k in range(peers):
            landed[k] = recv[c, k]
        return [landed[table[line, i]] for i in range(nodes)]

    halves = 2
    width = rows * NC // halves
    for half in range(halves):

        @pl.loop(0, nodes)
        def _(g):
            if half == 0:
                pltpu.make_async_copy(x_hbm.at[g], x.at[g], x_sem.at[g]).wait()
                pltpu.make_async_copy(col_basis.at[g], v.at[g], v_sem.at[g]).wait()
            leaf = lax.dot_general(
                x[g, :, half * width : (half + 1) * width], v[g],
                (((0,), (0,)), ((), ())), preferred_element_type=F32,
            ).astype(BF16)
            for e in range(NC // halves):
                first[half * (NC // halves) + e, g] = leaf[e * rows : (e + 1) * rows]

        if half == 0:
            pltpu.make_async_copy(w_col, w_col, w_sem.at[0]).wait()

        @pl.loop(half * (NC // halves), (half + 1) * (NC // halves))
        def _(c):
            states = mix([first[c, g] for g in range(nodes)], w_col)
            route(0, 0, states, x1_send, x1_recv, c)

    load_pairs(1, row_factors, w_row)

    def seek(g, origins):
        target = regroup[g]
        source = g // nodes
        hit = target // nodes == d
        place = lax.rem(target, nodes)
        return tuple(
            jnp.where(hit & (place == h), source, origin) for h, origin in enumerate(origins)
        )

    origins = lax.fori_loop(0, nodes * peers, seek, (jnp.int32(0),) * nodes)
    back_to = [lax.rem(origin - d + peers, peers) for origin in origins]
    for k in range(peers):
        table[2, k] = node_at(back_to, k)
    for h in range(nodes):
        table[1, h] = lax.rem(d - origins[h] + peers, peers)

    lines = contrast.shape[1] // rank
    contrast[...] = jnp.concatenate(
        [all_contrast[pl.ds(me * lines + i, 1)] for i in range(lines)], axis=1
    )
    pltpu.make_async_copy(w_row, w_row, w_sem.at[1]).wait()

    def phase2(c):
        wait_all(0, x1_send, x1_recv, c)
        states = mix(arrived(1, x1_recv, c), w_row)
        for h in range(nodes):
            z1_send[c, lax.rem(h - me + blocks, blocks)] = states[h]
        send_blk(1, z1_send, z1_recv, c)

    def phase3(c):
        wait_all(1, z1_send, z1_recv, c)
        states = jnp.concatenate([z1_recv[c, j] for j in range(blocks)], axis=1)
        basis = jnp.concatenate([u[j] for j in range(blocks)], axis=1)
        weighted = (contrast[...] * scale * matmul_t(states, basis)).astype(BF16)
        back = matmul(weighted, basis).astype(BF16)
        for j in range(blocks):
            z2_send[c, j] = back[:, j * rank : (j + 1) * rank]
        send_blk(2, z2_send, z2_recv, c)

    def phase4(c):
        wait_all(2, z2_send, z2_recv, c)
        states = unmix(
            [z2_recv[c, lax.rem(h - me + blocks, blocks)] for h in range(nodes)], w_row
        )
        route(3, 2, states, x2_send, x2_recv, c)

    def phase5(c, final_step):
        wait_all(3, x2_send, x2_recv, c)
        states = unmix(arrived(3, x2_recv, c), w_col, 1)

        @pl.when(final_step)
        def _():
            last = unmix_level(states, w_col, 0)
            for i in range(nodes):
                final[i, pl.ds(pl.multiple_of(c * rows, rows), rows)] = last[i]

        @pl.when(jnp.logical_not(final_step))
        def _():
            turned = list(states)
            for q, (h, p) in enumerate(pairs_of(1, nodes)):
                both = jnp.concatenate([states[h], states[p]], axis=1)
                out = matmul(both, w_turn[q]).astype(BF16)
                turned[h], turned[p] = out[:, :rank], out[:, rank:]
            route(0, 0, mix(turned, w_col, 1), x1_send, x1_recv, c)

    def turn():
        for q, pair in enumerate(pairs_of(1, nodes)):
            outer = w_col[0, q]
            halves = []
            for half, g in enumerate(pair):
                gram = lax.dot_general(
                    v[g], v[g], (((0,), (0,)), ((), ())), preferred_element_type=F32
                ).astype(BF16)
                halves.append(matmul(outer[:, half * rank : (half + 1) * rank], gram).astype(BF16))
            w_turn[q] = matmul_t(jnp.concatenate(halves, axis=1), outer).astype(BF16)

    codes = steps()
    first_sum = next(i for i, code in enumerate(codes) if code // 4 == 1)
    words = [
        sum(code << (BITS * i) for i, code in enumerate(codes[start : start + PER_WORD]))
        for start in range(0, len(codes), PER_WORD)
    ]

    @pl.loop(0, len(codes))
    def _(step):
        word = jnp.int32(words[0])
        for i, packed in enumerate(words[1:], 1):
            word = jnp.where(step >= i * PER_WORD, packed, word)
        shift = lax.rem(step, PER_WORD) * BITS
        code = lax.shift_right_logical(word, shift) & ((1 << BITS) - 1)
        kind = code // 4
        c = lax.rem(code, 4)

        @pl.when(kind == 0)
        def _():
            phase2(c)

        @pl.when(step == first_sum)
        def _():
            own_basis.wait()

            @pl.loop(1, blocks)
            def _(k):
                basis_copy(k).wait_send()
                basis_copy(blocks - k).wait_recv()

        @pl.when(kind == 1)
        def _():
            phase3(c)

        @pl.when(kind == 2)
        def _():
            phase4(c)

        @pl.when(code == TURN)
        def _():
            turn()

        @pl.when(code == FORWARD)
        def _():
            states = jnp.concatenate(
                [
                    jnp.concatenate([z1_recv[e, j] for j in range(blocks)], axis=1)
                    for e in range(NC)
                ],
                axis=0,
            )
            basis = jnp.concatenate([u[j] for j in range(blocks)], axis=1)
            forward[...] = (matmul_t(basis, states) * scale).astype(BF16)

        @pl.when((kind == 3) | (kind == 4))
        def _():
            phase5(c, kind == 4)


def expand_kernel(
    basis_hbm, state_hbm, sum_hbm, out_hbm, forward_hbm,
    basis, state, out, row_sum, in_sem, out_sem, sum_sem,
):
    nodes = basis.shape[0]

    def load(g):
        return (
            pltpu.make_async_copy(basis_hbm.at[g], basis.at[g], in_sem.at[0, g]),
            pltpu.make_async_copy(state_hbm.at[g], state.at[g], in_sem.at[1, g]),
        )

    def store(g):
        return pltpu.make_async_copy(out.at[g], out_hbm.at[g], out_sem.at[g])

    for g in range(nodes):
        for copy in load(g):
            copy.start()
    take = pltpu.make_async_copy(sum_hbm, row_sum, sum_sem.at[0])
    give = pltpu.make_async_copy(row_sum, forward_hbm, sum_sem.at[1])
    take.start()
    for g in range(nodes):
        if g == nodes // 2:
            take.wait()
            give.start()
        for copy in load(g):
            copy.wait()
        out[g] = matmul_t(basis[g], state[g]).astype(BF16)
        store(g).start()
    for g in range(nodes):
        store(g).wait()
    give.wait()


def shards(inputs, col_basis, col_factors, row_factors, row_basis, contrast, regroup):
    _, nodes, leaf, rank = col_basis.shape
    vectors = inputs.shape[-1]
    peers = lax.axis_size("bfly")
    blocks = lax.axis_size("blk")
    rows = vectors // NC
    hbm = pl.BlockSpec(memory_space=pl.ANY)
    vmem = pl.BlockSpec(memory_space=pltpu.VMEM)
    wide = (NC, peers, rows, rank)
    narrow = (NC, blocks, rows, rank)
    final, forward = pl.pallas_call(
        functools.partial(kernel, peers, blocks, blocks ** (-0.5)),
        out_shape=(
            jax.ShapeDtypeStruct((nodes, vectors, rank), BF16),
            jax.ShapeDtypeStruct((leaf, vectors), BF16),
        ),
        in_specs=[pl.BlockSpec(memory_space=pltpu.SMEM), hbm, hbm, hbm, hbm, hbm, vmem],
        out_specs=(vmem, vmem),
        scratch_shapes=[
            pltpu.VMEM((nodes, leaf, vectors), BF16),
            pltpu.VMEM((nodes, leaf, rank), BF16),
            pltpu.VMEM((blocks, leaf, rank), BF16),
            pltpu.VMEM((LEVELS, nodes // 2, 2 * rank, 2 * rank), BF16),
            pltpu.VMEM((LEVELS, nodes // 2, 2 * rank, 2 * rank), BF16),
            pltpu.VMEM((nodes // 2, 2 * rank, 2 * rank), BF16),
            pltpu.VMEM((1, leaf), F32),
            pltpu.VMEM((NC, nodes, rows, rank), BF16),
            pltpu.VMEM((nodes, rows, rank), BF16),
            pltpu.VMEM((peers, rows, rank), BF16),
            pltpu.SMEM((4, peers), jnp.int32),
            pltpu.VMEM(wide, BF16),
            pltpu.VMEM(wide, BF16),
            pltpu.VMEM(narrow, BF16),
            pltpu.VMEM(narrow, BF16),
            pltpu.VMEM(narrow, BF16),
            pltpu.VMEM(narrow, BF16),
            pltpu.VMEM(wide, BF16),
            pltpu.VMEM(wide, BF16),
            pltpu.SemaphoreType.DMA((nodes,)),
            pltpu.SemaphoreType.DMA((nodes,)),
            pltpu.SemaphoreType.DMA((2,)),
            pltpu.SemaphoreType.DMA,
            pltpu.SemaphoreType.DMA((blocks,)),
            pltpu.SemaphoreType.DMA((blocks,)),
            pltpu.SemaphoreType.DMA((4, NC)),
            pltpu.SemaphoreType.DMA((4, NC)),
        ],
        compiler_params=pltpu.CompilerParams(collective_id=0, has_side_effects=True),
        name="butterfly",
    )(
        regroup,
        inputs.reshape(nodes, leaf, vectors),
        col_basis[0],
        col_factors[0],
        row_factors[0],
        row_basis[0],
        contrast.reshape(-1, rank),
    )
    result, forward = pl.pallas_call(
        expand_kernel,
        out_shape=(
            jax.ShapeDtypeStruct((nodes, leaf, vectors), BF16),
            jax.ShapeDtypeStruct((leaf, vectors), BF16),
        ),
        in_specs=[hbm, hbm, hbm],
        out_specs=(hbm, hbm),
        scratch_shapes=[
            pltpu.VMEM((nodes, leaf, rank), BF16),
            pltpu.VMEM((nodes, vectors, rank), BF16),
            pltpu.VMEM((nodes, leaf, vectors), BF16),
            pltpu.VMEM((leaf, vectors), BF16),
            pltpu.SemaphoreType.DMA((2, nodes)),
            pltpu.SemaphoreType.DMA((nodes,)),
            pltpu.SemaphoreType.DMA((2,)),
        ],
        name="expand",
    )(col_basis[0], final, forward)
    return result.reshape(inputs.shape), forward


def solution(mesh):
    placed = (
        P("blk", "bfly", None),
        P("blk", "bfly", None, None),
        P("blk", "bfly", None, None, None),
        P("blk", "bfly", None, None, None),
        P("blk", "bfly", None, None),
        P("bfly"),
        P(),
    )
    return jax.shard_map(
        shards,
        mesh=mesh,
        in_specs=placed,
        out_specs=(P("blk", "bfly", None), P(("bfly", "blk"), None)),
        check_vma=False,
    )
```

```python
import functools

import jax
import jax.numpy as jnp
from jax import lax
from jax.experimental import pallas as pl
from jax.experimental.pallas import tpu as pltpu
from jax.sharding import PartitionSpec as P

LEVELS = 3
NC = 4
ORDER = (
    20, 21, 22, 30, 31, 32, 40, 23, 41, 42, 50, 33, 51, 43, 20, 52,
    21, 30, 53, 31, 40, 22, 41, 23, 32, 50, 33, 42, 43, 51, 20, 52,
    30, 53, 21, 40, 22, 31, 23, 32, 41, 33, 42, 43, 50, 51, 52, 53,
)
BITS = 5
PER_WORD = 6
FORWARD = 20
TURN = 24
BF16 = jnp.bfloat16
F32 = jnp.float32


def matmul(a, b):
    return lax.dot_general(a, b, (((1,), (0,)), ((), ())), preferred_element_type=F32)


def matmul_t(a, b):
    return lax.dot_general(a, b, (((1,), (1,)), ((), ())), preferred_element_type=F32)


def pairs_of(stride, nodes):
    return [(h, h + stride) for h in range(nodes) if not h & stride]


def mix_level(states, pair_matrices, level):
    states = list(states)
    for q, (h, p) in enumerate(pairs_of(1 << level, len(states))):
        both = jnp.concatenate([states[h], states[p]], axis=1)
        out = matmul_t(both, pair_matrices[level, q]).astype(BF16)
        rank = out.shape[1] // 2
        states[h], states[p] = out[:, :rank], out[:, rank:]
    return states


def unmix_level(states, pair_matrices, level):
    states = list(states)
    for q, (h, p) in enumerate(pairs_of(1 << level, len(states))):
        both = jnp.concatenate([states[h], states[p]], axis=1)
        out = matmul(both, pair_matrices[level, q]).astype(BF16)
        rank = out.shape[1] // 2
        states[h], states[p] = out[:, :rank], out[:, rank:]
    return states


def mix(states, pair_matrices, first=0):
    for level in range(first, LEVELS):
        states = mix_level(states, pair_matrices, level)
    return states


def unmix(states, pair_matrices, last=0):
    for level in reversed(range(last, LEVELS)):
        states = unmix_level(states, pair_matrices, level)
    return states


def node_at(offsets, k):
    place = jnp.int32(0)
    for i, offset in enumerate(offsets):
        place = jnp.where(offset == k, i, place)
    return place


def steps():
    codes = []
    for i, entry in enumerate(ORDER):
        phase, c = divmod(entry, 10)
        if phase == 5 and TURN not in codes:
            codes.append(TURN)
        left = ORDER[i + 1 :].count(entry)
        codes.append(4 * (phase - 2) + c + (4 if phase == 5 and not left else 0))
        if phase == 4 and not any(later // 10 == 4 for later in ORDER[i + 1 :]):
            codes.append(FORWARD)
    return codes


def kernel(
    peers, blocks, scale,
    regroup, x_hbm, col_basis, col_factors, row_factors, row_basis, all_contrast,
    final_hbm, forward_hbm,
    x, v, u, w_col, w_row, w_turn, contrast, first, held, landed, final, forward, table,
    x1_send, x1_recv, z1_send, z1_recv, z2_send, z2_recv, x2_send, x2_recv,
    x_sem, v_sem, w_sem, own_sem, u_send_sem, u_recv_sem, send_sem, recv_sem, out_sem,
):
    nodes = v.shape[0]
    rows = x1_send.shape[2]
    rank = x1_send.shape[3]
    d = lax.axis_index("bfly")
    me = lax.axis_index("blk")

    def bfly_peer(k):
        return {"bfly": lax.rem(d + k, peers)}

    def blk_peer(k):
        return {"blk": lax.rem(me + k, blocks)}

    barrier = pltpu.get_barrier_semaphore()

    @pl.loop(0, nodes)
    def _(g):
        pltpu.make_async_copy(x_hbm.at[g], x.at[g], x_sem.at[g]).start()
        pltpu.make_async_copy(col_basis.at[g], v.at[g], v_sem.at[g]).start()

    @pl.loop(1, peers)
    def _(k):
        pl.semaphore_signal(barrier, inc=1, device_id=bfly_peer(k))

    @pl.loop(1, blocks)
    def _(k):
        pl.semaphore_signal(barrier, inc=1, device_id=blk_peer(k))

    def load_pairs(which, source, target):
        for level in range(LEVELS):
            for q, (h, p) in enumerate(pairs_of(1 << level, nodes)):
                moves = (
                    (h, 0, 2 * rank, 0, 0), (p, 0, rank, rank, rank), (p, rank, rank, rank, 0)
                )
                for node, start, width, row, column in moves:
                    pltpu.make_async_copy(
                        source.at[node, level, :, pl.ds(start, width)],
                        target.at[level, q, pl.ds(row, rank), pl.ds(column, width)],
                        w_sem.at[which],
                    ).start()

    load_pairs(0, col_factors, w_col)
    own_basis = pltpu.make_async_copy(row_basis.at[me], u.at[0], own_sem)
    own_basis.start()

    owners = [regroup[d * nodes + i] // nodes for i in range(nodes)]
    there = [lax.rem(owner - d + peers, peers) for owner in owners]
    for k in range(peers):
        table[0, k] = node_at(there, k)
    for i in range(nodes):
        table[3, i] = lax.rem(d - owners[i] + peers, peers)

    pl.semaphore_wait(barrier, peers + blocks - 2)

    def basis_copy(k):
        target = lax.rem(me + k, blocks)
        return pltpu.make_async_remote_copy(
            src_ref=row_basis.at[target], dst_ref=u.at[blocks - k],
            send_sem=u_send_sem.at[k], recv_sem=u_recv_sem.at[blocks - k],
            device_id={"blk": target},
        )

    @pl.loop(1, blocks)
    def _(k):
        basis_copy(k).start()

    def send_bfly(which, send, recv, c):
        @pl.loop(1, peers)
        def _(k):
            pltpu.make_async_remote_copy(
                src_ref=send.at[c, k], dst_ref=recv.at[c, k],
                send_sem=send_sem.at[which, c], recv_sem=recv_sem.at[which, c],
                device_id=bfly_peer(k),
            ).start()

    def send_blk(which, send, recv, c):
        recv[c, 0] = send[c, 0]

        @pl.loop(1, blocks)
        def _(k):
            pltpu.make_async_remote_copy(
                src_ref=send.at[c, k], dst_ref=recv.at[c, blocks - k],
                send_sem=send_sem.at[which, c], recv_sem=recv_sem.at[which, c],
                device_id=blk_peer(k),
            ).start()

    def wait_all(which, send, recv, c):
        count = send.shape[1] - 1
        part = recv.at[c, pl.ds(1, count)]
        pltpu.make_async_copy(part, part, recv_sem.at[which, c]).wait()
        part = send.at[c, pl.ds(1, count)]
        pltpu.make_async_copy(part, part, send_sem.at[which, c]).wait()

    def route(which, line, states, send, recv, c):
        for i, state in enumerate(states):
            held[i] = state
        recv[c, 0] = held[table[line, 0]]
        for k in range(1, peers):
            send[c, k] = held[table[line, k]]
        send_bfly(which, send, recv, c)

    def arrived(line, recv, c):
        for k in range(peers):
            landed[k] = recv[c, k]
        return [landed[table[line, i]] for i in range(nodes)]

    halves = 2
    width = rows * NC // halves
    for half in range(halves):

        @pl.loop(0, nodes)
        def _(g):
            if half == 0:
                pltpu.make_async_copy(x_hbm.at[g], x.at[g], x_sem.at[g]).wait()
                pltpu.make_async_copy(col_basis.at[g], v.at[g], v_sem.at[g]).wait()
            leaf = lax.dot_general(
                x[g, :, half * width : (half + 1) * width], v[g],
                (((0,), (0,)), ((), ())), preferred_element_type=F32,
            ).astype(BF16)
            for e in range(NC // halves):
                first[half * (NC // halves) + e, g] = leaf[e * rows : (e + 1) * rows]

        if half == 0:
            pltpu.make_async_copy(w_col, w_col, w_sem.at[0]).wait()

        @pl.loop(half * (NC // halves), (half + 1) * (NC // halves))
        def _(c):
            states = mix([first[c, g] for g in range(nodes)], w_col)
            route(0, 0, states, x1_send, x1_recv, c)

    load_pairs(1, row_factors, w_row)

    def seek(g, origins):
        target = regroup[g] - d * nodes
        source = g // nodes
        return tuple(jnp.where(target == h, source, origin) for h, origin in enumerate(origins))

    origins = lax.fori_loop(0, nodes * peers, seek, (jnp.int32(0),) * nodes, unroll=nodes)
    back_to = [lax.rem(origin - d + peers, peers) for origin in origins]
    for k in range(peers):
        table[2, k] = node_at(back_to, k)
    for h in range(nodes):
        table[1, h] = lax.rem(d - origins[h] + peers, peers)

    lines = contrast.shape[1] // rank
    contrast[...] = jnp.concatenate(
        [all_contrast[pl.ds(me * lines + i, 1)] for i in range(lines)], axis=1
    )
    pltpu.make_async_copy(w_row, w_row, w_sem.at[1]).wait()

    def phase2(c):
        wait_all(0, x1_send, x1_recv, c)
        states = mix(arrived(1, x1_recv, c), w_row)
        for h in range(nodes):
            z1_send[c, lax.rem(h - me + blocks, blocks)] = states[h]
        send_blk(1, z1_send, z1_recv, c)

    def phase3(c):
        wait_all(1, z1_send, z1_recv, c)
        states = jnp.concatenate([z1_recv[c, j] for j in range(blocks)], axis=1)
        basis = jnp.concatenate([u[j] for j in range(blocks)], axis=1)
        weighted = (contrast[...] * scale * matmul_t(states, basis)).astype(BF16)
        back = matmul(weighted, basis).astype(BF16)
        for j in range(blocks):
            z2_send[c, j] = back[:, j * rank : (j + 1) * rank]
        send_blk(2, z2_send, z2_recv, c)

    def phase4(c):
        wait_all(2, z2_send, z2_recv, c)
        states = unmix(
            [z2_recv[c, lax.rem(h - me + blocks, blocks)] for h in range(nodes)], w_row
        )
        route(3, 2, states, x2_send, x2_recv, c)

    def phase5(c, final_step):
        wait_all(3, x2_send, x2_recv, c)
        states = unmix(arrived(3, x2_recv, c), w_col, 1)

        @pl.when(final_step)
        def _():
            last = unmix_level(states, w_col, 0)
            for i in range(nodes):
                final[c, i] = last[i]
            give_final(c).start()

        @pl.when(jnp.logical_not(final_step))
        def _():
            turned = list(states)
            for q, (h, p) in enumerate(pairs_of(1, nodes)):
                both = jnp.concatenate([states[h], states[p]], axis=1)
                out = matmul(both, w_turn[q]).astype(BF16)
                turned[h], turned[p] = out[:, :rank], out[:, rank:]
            route(0, 0, mix(turned, w_col, 1), x1_send, x1_recv, c)

    def turn():
        for q, pair in enumerate(pairs_of(1, nodes)):
            outer = w_col[0, q]
            halves = []
            for half, g in enumerate(pair):
                gram = lax.dot_general(
                    v[g], v[g], (((0,), (0,)), ((), ())), preferred_element_type=F32
                ).astype(BF16)
                halves.append(matmul(outer[:, half * rank : (half + 1) * rank], gram).astype(BF16))
            w_turn[q] = matmul_t(jnp.concatenate(halves, axis=1), outer).astype(BF16)

    def give_final(c):
        span = pl.ds(pl.multiple_of(c * rows, rows), rows)
        return pltpu.make_async_copy(final.at[c], final_hbm.at[:, span], out_sem.at[c])

    give_forward = pltpu.make_async_copy(forward, forward_hbm, out_sem.at[NC])
    codes = steps()
    first_sum = next(i for i, code in enumerate(codes) if code // 4 == 1)
    words = [
        sum(code << (BITS * i) for i, code in enumerate(codes[start : start + PER_WORD]))
        for start in range(0, len(codes), PER_WORD)
    ]

    @pl.loop(0, len(codes))
    def _(step):
        word = jnp.int32(words[0])
        for i, packed in enumerate(words[1:], 1):
            word = jnp.where(step >= i * PER_WORD, packed, word)
        shift = lax.rem(step, PER_WORD) * BITS
        code = lax.shift_right_logical(word, shift) & ((1 << BITS) - 1)
        kind = code // 4
        c = lax.rem(code, 4)

        @pl.when(kind == 0)
        def _():
            phase2(c)

        @pl.when(step == first_sum)
        def _():
            own_basis.wait()

            @pl.loop(1, blocks)
            def _(k):
                basis_copy(k).wait_send()
                basis_copy(blocks - k).wait_recv()

        @pl.when(kind == 1)
        def _():
            phase3(c)

        @pl.when(kind == 2)
        def _():
            phase4(c)

        @pl.when(code == TURN)
        def _():
            turn()

        @pl.when(code == FORWARD)
        def _():
            states = jnp.concatenate(
                [
                    jnp.concatenate([z1_recv[e, j] for j in range(blocks)], axis=1)
                    for e in range(NC)
                ],
                axis=0,
            )
            basis = jnp.concatenate([u[j] for j in range(blocks)], axis=1)
            forward[...] = (matmul_t(basis, states) * scale).astype(BF16)
            give_forward.start()

        @pl.when((kind == 3) | (kind == 4))
        def _():
            phase5(c, kind == 4)

    give_forward.wait()

    @pl.loop(0, NC)
    def _(c):
        give_final(c).wait()


def expand_kernel(
    basis_hbm, state_hbm, sum_hbm, out_hbm, forward_hbm,
    basis, state, out, row_sum, in_sem, out_sem, sum_sem,
):
    nodes = basis.shape[0]

    def load(g):
        return (
            pltpu.make_async_copy(basis_hbm.at[g], basis.at[g], in_sem.at[0, g]),
            pltpu.make_async_copy(state_hbm.at[g], state.at[g], in_sem.at[1, g]),
        )

    def store(g):
        return pltpu.make_async_copy(out.at[g], out_hbm.at[g], out_sem.at[g])

    for g in range(nodes):
        for copy in load(g):
            copy.start()
    take = pltpu.make_async_copy(sum_hbm, row_sum, sum_sem.at[0])
    give = pltpu.make_async_copy(row_sum, forward_hbm, sum_sem.at[1])
    take.start()
    for g in range(nodes):
        if g == nodes // 2:
            take.wait()
            give.start()
        for copy in load(g):
            copy.wait()
        out[g] = matmul_t(basis[g], state[g]).astype(BF16)
        store(g).start()
    for g in range(nodes):
        store(g).wait()
    give.wait()


def shards(inputs, col_basis, col_factors, row_factors, row_basis, contrast, regroup):
    _, nodes, leaf, rank = col_basis.shape
    vectors = inputs.shape[-1]
    peers = lax.axis_size("bfly")
    blocks = lax.axis_size("blk")
    rows = vectors // NC
    hbm = pl.BlockSpec(memory_space=pl.ANY)
    vmem = pl.BlockSpec(memory_space=pltpu.VMEM)
    wide = (NC, peers, rows, rank)
    narrow = (NC, blocks, rows, rank)
    final, forward = pl.pallas_call(
        functools.partial(kernel, peers, blocks, blocks ** (-0.5)),
        out_shape=(
            jax.ShapeDtypeStruct((nodes, vectors, rank), BF16),
            jax.ShapeDtypeStruct((leaf, vectors), BF16),
        ),
        in_specs=[pl.BlockSpec(memory_space=pltpu.SMEM), hbm, hbm, hbm, hbm, hbm, vmem],
        out_specs=(hbm, hbm),
        scratch_shapes=[
            pltpu.VMEM((nodes, leaf, vectors), BF16),
            pltpu.VMEM((nodes, leaf, rank), BF16),
            pltpu.VMEM((blocks, leaf, rank), BF16),
            pltpu.VMEM((LEVELS, nodes // 2, 2 * rank, 2 * rank), BF16),
            pltpu.VMEM((LEVELS, nodes // 2, 2 * rank, 2 * rank), BF16),
            pltpu.VMEM((nodes // 2, 2 * rank, 2 * rank), BF16),
            pltpu.VMEM((1, leaf), F32),
            pltpu.VMEM((NC, nodes, rows, rank), BF16),
            pltpu.VMEM((nodes, rows, rank), BF16),
            pltpu.VMEM((peers, rows, rank), BF16),
            pltpu.VMEM((NC, nodes, rows, rank), BF16),
            pltpu.VMEM((leaf, vectors), BF16),
            pltpu.SMEM((4, peers), jnp.int32),
            pltpu.VMEM(wide, BF16),
            pltpu.VMEM(wide, BF16),
            pltpu.VMEM(narrow, BF16),
            pltpu.VMEM(narrow, BF16),
            pltpu.VMEM(narrow, BF16),
            pltpu.VMEM(narrow, BF16),
            pltpu.VMEM(wide, BF16),
            pltpu.VMEM(wide, BF16),
            pltpu.SemaphoreType.DMA((nodes,)),
            pltpu.SemaphoreType.DMA((nodes,)),
            pltpu.SemaphoreType.DMA((2,)),
            pltpu.SemaphoreType.DMA,
            pltpu.SemaphoreType.DMA((blocks,)),
            pltpu.SemaphoreType.DMA((blocks,)),
            pltpu.SemaphoreType.DMA((4, NC)),
            pltpu.SemaphoreType.DMA((4, NC)),
            pltpu.SemaphoreType.DMA((NC + 1,)),
        ],
        compiler_params=pltpu.CompilerParams(collective_id=0, has_side_effects=True),
        name="butterfly",
    )(
        regroup,
        inputs.reshape(nodes, leaf, vectors),
        col_basis[0],
        col_factors[0],
        row_factors[0],
        row_basis[0],
        contrast.reshape(-1, rank),
    )
    result, forward = pl.pallas_call(
        expand_kernel,
        out_shape=(
            jax.ShapeDtypeStruct((nodes, leaf, vectors), BF16),
            jax.ShapeDtypeStruct((leaf, vectors), BF16),
        ),
        in_specs=[hbm, hbm, hbm],
        out_specs=(hbm, hbm),
        scratch_shapes=[
            pltpu.VMEM((nodes, leaf, rank), BF16),
            pltpu.VMEM((nodes, vectors, rank), BF16),
            pltpu.VMEM((nodes, leaf, vectors), BF16),
            pltpu.VMEM((leaf, vectors), BF16),
            pltpu.SemaphoreType.DMA((2, nodes)),
            pltpu.SemaphoreType.DMA((nodes,)),
            pltpu.SemaphoreType.DMA((2,)),
        ],
        name="expand",
    )(col_basis[0], final, forward)
    return result.reshape(inputs.shape), forward


def solution(mesh):
    placed = (
        P("blk", "bfly", None),
        P("blk", "bfly", None, None),
        P("blk", "bfly", None, None, None),
        P("blk", "bfly", None, None, None),
        P("blk", "bfly", None, None),
        P("bfly"),
        P(),
    )
    return jax.shard_map(
        shards,
        mesh=mesh,
        in_specs=placed,
        out_specs=(P("blk", "bfly", None), P(("bfly", "blk"), None)),
        check_vma=False,
    )
```
